1024 devices in a mesh: ctx: 64 (over z, x), tp: 16 (over y, core).
Axes of the slice: x: 4, y: 8, z: 16, core: 2. Of those that a mesh axis runs over, the one named last changes fastest.
Arguments:
- gate_q: bfloat16 [4096, 16384], P('tp', 'ctx'), may hold values from -6 to 6
- key_k: bfloat16 [4096, 16384], P('tp', 'ctx'), may hold values from -6 to 6
- value_v: bfloat16 [4096, 16384], P('tp', 'ctx'), may hold values from -6 to 6
- filter_taps: float32 [4096, 16384], P('tp', 'ctx'), may hold values from -1 to 1
- skip_bias: float32 [4096], P('tp'), may hold values from 0.5 to 1.5
- w_out: bfloat16 [4096, 4096], P('tp'), may hold values from -0.125 to 0.125
Outputs:
- mixed: bfloat16 [4096, 16384], P('tp', 'ctx')
The draws below stay inside these ranges and needn't reach their ends.
All inputs are finite; a program needn't handle non-finite values.
Results may differ from the reference program's by a relative error of at most 0.018.
Values may be sent and summed in bfloat16 or wider, within the bound.
A program may use at most 32 MiB of HBM per device.

```python
import math
import jax
import jax.numpy as jnp
from jax import lax

CH_DEV = 256
D = 4096
SEQ = 16384
CHANNELS = 4096
N_TP = 16


def draw_filter_taps(key, part):
    key_pick, key_slow, key_fast, key_rough = jax.random.split(key, 4)
    slow_share = 5
    chosen = jax.random.randint(key_pick, (CHANNELS, 1), 0, 10) < slow_share
    slow_tau = SEQ * jnp.exp(jax.random.uniform(key_slow, (CHANNELS, 1), minval=0.0, maxval=math.log(8.0)))
    fast_tau = jax.random.uniform(key_fast, (CHANNELS, 1), minval=30.0, maxval=50.0)
    decay_len = jnp.where(chosen, slow_tau, fast_tau)
    positions = jnp.arange(SEQ, dtype=jnp.float32)[None, :]
    rough = jnp.clip(jax.random.normal(key_rough, (CHANNELS, SEQ)), -4.0, 4.0)
    scale_rows = 1.0 / jnp.sqrt(jnp.minimum(decay_len, SEQ * 1.0))
    return (rough * jnp.exp(-positions / decay_len) * scale_rows).astype(jnp.float32)


def strengthened(result, rng, source, target, blocks, factor):
    def block_of(axis_at):
        return (jnp.arange(result.shape[axis_at]) // (result.shape[axis_at] // blocks)).reshape((-1,) + (1,) * (result.ndim - 1 - axis_at))

    first = jax.random.permutation(rng, blocks)[block_of(target)]
    other_side = (block_of(target) + blocks // 2) % blocks
    return jnp.where((block_of(source) == first) | (block_of(source) == other_side), factor * result, result)


def block_scale(own_key, extent, shards, least, largest):
    loudness, own = 1.0, jax.random.fold_in(own_key, 6)
    for position, shards_of in shards:
        heights = jnp.exp(jax.random.uniform(jax.random.fold_in(own, position), (shards_of,), jnp.float32, least / len(shards), largest / len(shards)))
        loudness = loudness * jnp.repeat(heights, extent[position] // shards_of).reshape([-1 if axis == position else 1 for axis in range(len(extent))])
    return loudness


def bell_draw(stream_key, extent, deviation, most, cuts=(), held_as=jnp.bfloat16):
    array = deviation * jax.random.normal(stream_key, extent, jnp.float32)
    if cuts:
        array = array * block_scale(stream_key, extent, cuts, -0.22, 0.18)
    return jnp.clip(array, -most, most).astype(held_as)


def gaussian_with(stream_key, extent, width, most, cuts, heavy, kind=jnp.bfloat16):
    entries = width * jax.random.normal(stream_key, extent, jnp.float32)
    if cuts:
        entries = entries * block_scale(stream_key, extent, cuts, -0.22, 0.18)
    return jnp.clip(strengthened(entries, jax.random.fold_in(stream_key, 3), *heavy), -most, most).astype(kind)


def setup_inputs(seed: int = 0) -> dict:
    key_of = jax.random.split(jax.random.key(seed), 7)
    gate_q = bell_draw(key_of[0], (CHANNELS, SEQ), 1.0, 6.0, ((0, 16), (1, 64)))
    key_k = bell_draw(key_of[1], (CHANNELS, SEQ), 1.0, 6.0, ((0, 16), (1, 64)))
    value_v = bell_draw(key_of[2], (CHANNELS, SEQ), 1.0, 6.0, ((0, 16), (1, 64)))
    filter_taps = draw_filter_taps(jax.random.fold_in(key_of[6], 71), 0)
    skip_bias = jnp.clip(0.5 + 1.0 * jax.random.uniform(key_of[4], (CHANNELS,), jnp.float32) ** block_scale(key_of[4], (CHANNELS,), ((0, 16),), -0.2, 0.2), 0.5, 1.5)
    w_out = gaussian_with(key_of[5], (CHANNELS, D), CHANNELS ** -0.5, 0.125, ((0, 16),), (0, 1, 16, 2.0))
    return {"gate_q": gate_q, "key_k": key_k, "value_v": value_v, "filter_taps": filter_taps, "skip_bias": skip_bias, "w_out": w_out}


def reference(gate_q, key_k, value_v, filter_taps, skip_bias, w_out):
    length = 2 * SEQ

    def add_block(running, block_id):
        first_row = (block_id * CH_DEV).astype(jnp.int32)
        gate_rows = lax.dynamic_slice_in_dim(gate_q, first_row, CH_DEV, 0).astype(jnp.float32)
        key_rows = lax.dynamic_slice_in_dim(key_k, first_row, CH_DEV, 0).astype(jnp.float32)
        value_rows = lax.dynamic_slice_in_dim(value_v, first_row, CH_DEV, 0).astype(jnp.float32)
        tap_rows = lax.dynamic_slice_in_dim(filter_taps, first_row, CH_DEV, 0)
        bias_rows = lax.dynamic_slice_in_dim(skip_bias, first_row, CH_DEV, 0)
        weight = lax.dynamic_slice_in_dim(w_out, first_row, CH_DEV, 0)
        signal = key_rows * value_rows
        spectrum = jnp.fft.rfft(signal, n=length, axis=1) * jnp.fft.rfft(tap_rows, n=length, axis=1)
        convolved = jnp.fft.irfft(spectrum, n=length, axis=1)[:, :SEQ]
        gated_vals = (gate_rows * (convolved + bias_rows[:, None] * signal)).astype(jnp.bfloat16)
        partial_value = lax.dot_general(weight, gated_vals, (((0,), (0,)), ((), ())), preferred_element_type=jnp.float32)
        partial_value = partial_value.astype(jnp.bfloat16)
        return running + partial_value.astype(jnp.float32), None

    running, _ = lax.scan(add_block, jnp.zeros((D, SEQ), jnp.float32), jnp.arange(N_TP, dtype=jnp.int32))
    return running.astype(jnp.bfloat16)
```

```python
import math

import jax
import jax.numpy as jnp
import numpy as np
from jax import lax
from jax.sharding import PartitionSpec as P

TOP = lax.Precision.HIGHEST
R = 128


def tables():
    length = R * R
    row = np.arange(R)
    shifted = row - 0.25
    first = 2.0 * np.pi * np.outer(shifted, row) / R
    twist = 2.0 * np.pi * np.outer(shifted, row) / length
    second = 2.0 * np.pi * np.outer(row, row) / R
    forward_a = np.stack([np.cos(first), -np.sin(first)])
    forward_b = np.block(
        [[np.cos(second), -np.sin(second)], [np.sin(second), np.cos(second)]]
    )
    back_b = forward_b.T
    back_a = np.stack([np.cos(first).T, -np.sin(first).T]) / length
    as32 = lambda t: np.asarray(t, np.float32)
    return tuple(map(as32, (forward_a, np.cos(twist), np.sin(twist), forward_b, back_b, back_a)))


def convolve(pair):
    forward_a, cos_t, sin_t, forward_b, back_b, back_a = tables()
    grid = pair.astype(jnp.float32).reshape(2, pair.shape[1], R, R)
    mid = jnp.einsum("rka,scab->rsckb", forward_a, grid, precision=TOP)
    re, im = mid[0], mid[1]
    mid = jnp.concatenate([re * cos_t + im * sin_t, im * cos_t - re * sin_t], axis=-1)
    spec = jnp.einsum("sckb,bm->sckm", mid, forward_b, precision=TOP)
    re, im = spec[..., :R], spec[..., R:]
    prod = jnp.concatenate([re[0] * re[1] - im[0] * im[1], re[0] * im[1] + im[0] * re[1]], axis=-1)
    mid = jnp.einsum("ckm,mb->ckb", prod, back_b, precision=TOP)
    re, im = mid[..., :R], mid[..., R:]
    re, im = re * cos_t - im * sin_t, im * cos_t + re * sin_t
    out = jnp.einsum("ak,ckb->cab", back_a[0], re, precision=TOP)
    out = out + jnp.einsum("ak,ckb->cab", back_a[1], im, precision=TOP)
    return out.reshape(out.shape[0], R * R)


def body(gate_q, key_k, value_v, filter_taps, skip_bias, w_out):
    signal = key_k.astype(jnp.float32) * value_v.astype(jnp.float32)
    pair = jnp.stack([signal.astype(jnp.bfloat16), filter_taps.astype(jnp.bfloat16)])
    pair = lax.all_to_all(pair, "ctx", split_axis=1, concat_axis=2, tiled=True)
    values = convolve(pair).astype(jnp.bfloat16)
    convolved = lax.all_to_all(values, "ctx", split_axis=1, concat_axis=0, tiled=True)
    gated_vals = (
        gate_q.astype(jnp.float32)
        * (convolved.astype(jnp.float32) + skip_bias[:, None] * signal)
    ).astype(jnp.bfloat16)
    return lax.psum_scatter(
        lax.dot_general(
            w_out, gated_vals, (((0,), (0,)), ((), ())), preferred_element_type=jnp.float32
        ).astype(jnp.bfloat16),
        "tp",
        scatter_dimension=0,
        tiled=True,
    )


def solution(mesh):
    return jax.shard_map(
        body,
        mesh=mesh,
        in_specs=(
            P("tp", "ctx"),
            P("tp", "ctx"),
            P("tp", "ctx"),
            P("tp", "ctx"),
            P("tp"),
            P("tp", None),
        ),
        out_specs=P("tp", "ctx"),
        check_vma=False,
    )
```

```python
import functools

import jax
import jax.numpy as jnp
import ml_dtypes
import numpy as np
from jax import lax
from jax.experimental import pallas as pl
from jax.experimental.pallas import tpu as pltpu
from jax.sharding import PartitionSpec as P

MESH = pl.DeviceIdType.MESH
F32 = jnp.float32
BF16 = jnp.bfloat16
NX = 4


def split_np(table):
    high = np.asarray(table, np.float32).astype(ml_dtypes.bfloat16)
    low = (table - high.astype(np.float64)).astype(ml_dtypes.bfloat16)
    return [high, low]


def tables(nz, nx, own, width):
    shards = nz * nx
    length = shards * width
    freq = np.arange(shards) - 0.25
    block = np.array([z * nx + x for x in range(nx) for z in range(nz)])
    first = 2.0 * np.pi * np.outer(freq, block) / shards
    eye = np.eye(own)
    spread = lambda m: np.einsum("ki,cd->ckid", m, eye).reshape(own * shards, shards * own)
    ahead = np.stack(split_np(spread(np.cos(first))) + split_np(spread(-np.sin(first))))
    back = np.stack(
        split_np(spread(np.cos(first)).T / length) + split_np(spread(-np.sin(first)).T / length)
    )
    angle = 2.0 * np.pi * np.outer(freq, np.arange(width)) / length
    twist = np.stack([np.cos(angle), np.sin(angle)]).astype(np.float32)
    angle = 2.0 * np.pi * (np.outer(np.arange(width), np.arange(width)) % width) / width
    inner = np.stack(split_np(np.cos(angle)) + split_np(np.sin(angle)))
    rows = shards * own
    order = np.arange(rows).reshape(nz, nx, own).transpose(1, 0, 2).reshape(-1)
    to_x = np.zeros((rows, rows))
    to_x[np.arange(rows), order] = 1.0
    perm = np.stack([to_x, to_x.T]).astype(ml_dtypes.bfloat16)
    return ahead, back, twist, inner, perm


def dot(a, b):
    return jnp.dot(a, b, preferred_element_type=F32)


def split(a):
    high = a.astype(BF16)
    return high, (a - high.astype(F32)).astype(BF16)


def dot3(a, b):
    return dot(a[0], b[0]) + (dot(a[0], b[1]) + dot(a[1], b[0]))


def kernel(
    nz, nx, ny,
    gate, key, value, taps, skip, w, ahead, back, twist, inner, perm,
    out,
    sig, skip_cols, w_t, zsend, zbuf, xsend, xbuf, spec, csend, cbuf, dsend, conv,
    psend, precv, own, rsend, rrecv,
    zs_sem, zr_sem, xs_sem, xr_sem, ps_sem, pr_sem, rs_sem, rr_sem,
):
    channels, width = key.shape
    shards = nz * nx
    mine = channels // shards
    zrows = nx * mine
    xrows = nz * mine
    drows = out.shape[0]
    half = width // 2
    ctx = lax.axis_index("ctx")
    tp = lax.axis_index("tp")
    z, x = ctx // nx, ctx % nx
    y, core = tp // 2, tp % 2

    def z_at(o):
        return (z + o + nz) % nz

    def x_at(o):
        return (x + o) % nx

    def y_at(o):
        return (y + o + ny) % ny

    def z_peer(o):
        return {"ctx": z_at(o) * nx + x}

    def x_peer(o):
        return {"ctx": z * nx + x_at(o)}

    def y_peer(o):
        return {"tp": y_at(o) * 2 + core}

    partner = {"tp": y * 2 + (1 - core)}
    z_order = [nz // 2]
    for o in range(nz // 2 - 1, 0, -1):
        z_order += [o, -o]
    x_order = list(range(1, nx))

    barrier = pltpu.get_barrier_semaphore()
    peers = [z_peer(o) for o in z_order] + [x_peer(o) for o in x_order]
    peers += [partner, y_peer(1), y_peer(-1)]
    for peer in peers:
        pl.semaphore_signal(barrier, inc=1, device_id=peer, device_id_type=MESH)

    started = []

    def rows_z(i):
        return pl.ds(pl.multiple_of(i * zrows, zrows), zrows)

    def rows_x(i):
        return pl.ds(pl.multiple_of(i * xrows, xrows), xrows)

    def z_copy(kind, source, target, n, o):
        return pltpu.make_async_remote_copy(
            src_ref=source.at[rows_z(z_at(o))],
            dst_ref=target.at[rows_z(z)],
            send_sem=zs_sem.at[kind, n],
            recv_sem=zr_sem.at[kind, n],
            device_id=z_peer(o),
            device_id_type=MESH,
        )

    def x_copy(kind, source, target, n, o):
        return pltpu.make_async_remote_copy(
            src_ref=source.at[rows_x(x_at(o))],
            dst_ref=target.at[rows_x(x)],
            send_sem=xs_sem.at[kind, n],
            recv_sem=xr_sem.at[kind, n],
            device_id=x_peer(o),
            device_id_type=MESH,
        )

    def z_start(kind, source, target):
        copies = [z_copy(kind, source, target, n, o) for n, o in enumerate(z_order)]
        for copy in copies:
            copy.start()
        target[rows_z(z), :] = source[rows_z(z), :]
        started.extend(copies)
        return copies

    def x_start(kind, source, target):
        copies = [x_copy(kind, source, target, n, o) for n, o in enumerate(x_order)]
        for copy in copies:
            copy.start()
        target[rows_x(x), :] = source[rows_x(x), :]
        started.extend(copies)
        return copies

    def arrive(copies):
        for copy in copies:
            copy.wait_recv()

    tall = lambda t: jnp.concatenate([t] * mine, axis=0)

    def forward(rows):
        re = dot(ahead[0], rows) + dot(ahead[1], rows)
        im = dot(ahead[2], rows) + dot(ahead[3], rows)
        cos_t, sin_t = tall(twist[0]), tall(twist[1])
        mid_re, mid_im = split(re * cos_t + im * sin_t), split(im * cos_t - re * sin_t)
        cos_p, sin_p = (inner[0], inner[1]), (inner[2], inner[3])
        return (
            dot3(mid_re, cos_p) + dot3(mid_im, sin_p),
            dot3(mid_im, cos_p) - dot3(mid_re, sin_p),
        )

    zsend[0] = taps[...].astype(BF16)
    pl.semaphore_wait(barrier, len(peers))
    taps_z = z_start(0, zsend.at[0], zbuf.at[0])
    sig[...] = key[...].astype(F32) * value[...].astype(F32)
    zsend[1] = sig[...].astype(BF16)
    sig_z = z_start(1, zsend.at[1], zbuf.at[1])

    skip_cols[...] = jnp.broadcast_to(skip[...], (width, channels)).T
    for j in range(w.shape[1] // drows):
        w_t[pl.ds(j * drows, drows), :] = w[:, pl.ds(j * drows, drows)].T

    arrive(taps_z)
    xsend[0] = dot(perm[0], zbuf[0]).astype(BF16)
    taps_x = x_start(0, xsend.at[0], xbuf.at[0])
    arrive(taps_x)
    spec_re, spec_im = forward(xbuf[0])
    spec[0] = spec_re
    spec[1] = spec_im
    arrive(sig_z)
    xsend[1] = dot(perm[0], zbuf[1]).astype(BF16)
    sig_x = x_start(1, xsend.at[1], xbuf.at[1])
    arrive(sig_x)

    sre, sim = forward(xbuf[1])
    tre, tim = spec[0], spec[1]
    pre, pim = split(sre * tre - sim * tim), split(sre * tim + sim * tre)
    cos_p, sin_p = (inner[0], inner[1]), (inner[2], inner[3])
    re = dot3(pre, cos_p) - dot3(pim, sin_p)
    im = dot3(pim, cos_p) + dot3(pre, sin_p)
    cos_t, sin_t = tall(twist[0]), tall(twist[1])
    re, im = split(re * cos_t - im * sin_t), split(im * cos_t + re * sin_t)
    csend[...] = (dot3((back[0], back[1]), re) + dot3((back[2], back[3]), im)).astype(BF16)

    conv_x = x_start(2, csend, cbuf)
    arrive(conv_x)
    dsend[...] = dot(perm[1], cbuf[...]).astype(BF16)
    conv_z = z_start(2, dsend, conv)
    arrive(conv_z)

    gated = (
        gate[...].astype(F32) * (conv[...].astype(F32) + skip_cols[...] * sig[...])
    ).astype(BF16)

    reach = ny // 2
    offsets = [reach]
    for o in range(reach - 1, 0, -1):
        offsets += [o, -o]
    offsets += [0]
    slot = {o: n for n, o in enumerate(offsets)}
    slot[-reach] = 0

    def weight_rows(o, side):
        return w_t[pl.ds(pl.multiple_of((y_at(o) * 2 + side) * drows, drows), drows), :]

    pair = []
    for n, o in enumerate(offsets):
        psend[n] = dot(weight_rows(o, 1 - core), gated).astype(BF16)
        copy = pltpu.make_async_remote_copy(
            src_ref=psend.at[n],
            dst_ref=precv.at[n],
            send_sem=ps_sem.at[n],
            recv_sem=pr_sem.at[n],
            device_id=partner,
            device_id_type=MESH,
        )
        copy.start()
        pair.append(copy)
        own[n] = dot(weight_rows(o, core), gated)
    started.extend(pair)

    there = set()

    def chip_sum(o, lanes):
        n = slot[o]
        if n not in there:
            pair[n].wait_recv()
            there.add(n)
        return own[n, :, lanes] + precv[n, :, lanes].astype(F32)

    low, high = pl.ds(0, half), pl.ds(half, half)
    rings = [(1, low, reach), (-1, high, reach), (1, high, reach - 1), (-1, low, reach - 1)]
    last = [None] * len(rings)
    for step in range(reach):
        for r, (way, lanes, begin) in enumerate(rings):
            distance = begin - step
            if distance < 1:
                continue
            total = chip_sum(way * distance, lanes)
            if last[r] is not None:
                last[r].wait_recv()
                total = total + rrecv[r, step - 1].astype(F32)
            rsend[r, step] = total.astype(BF16)
            copy = pltpu.make_async_remote_copy(
                src_ref=rsend.at[r, step],
                dst_ref=rrecv.at[r, step],
                send_sem=rs_sem.at[r, step],
                recv_sem=rr_sem.at[r, step],
                device_id=y_peer(way),
                device_id_type=MESH,
            )
            copy.start()
            started.append(copy)
            last[r] = copy
    for lanes, ends in ((low, (0, 3)), (high, (1, 2))):
        total = chip_sum(0, lanes)
        for r in ends:
            if last[r] is not None:
                last[r].wait_recv()
                total = total + rrecv[r, rings[r][2] - 1].astype(F32)
        out[:, lanes] = total.astype(BF16)

    for copy in started:
        copy.wait_send()


def body(nz, nx, ny, gate_q, key_k, value_v, filter_taps, skip_bias, w_out):
    channels, width = key_k.shape
    depth = w_out.shape[1]
    drows = depth // (2 * ny)
    reach = ny // 2
    consts = tables(nz, nx, channels // (nz * nx), width)
    vmem = lambda *shape, dtype=BF16: pltpu.VMEM(shape, dtype)
    dma = lambda *shape: pltpu.SemaphoreType.DMA(shape)
    scratch = [
        vmem(channels, width, dtype=F32),
        vmem(channels, width, dtype=F32),
        vmem(depth, channels),
        vmem(2, channels, width),
        vmem(2, channels, width),
        vmem(2, channels, width),
        vmem(2, channels, width),
        vmem(2, channels, width, dtype=F32),
        vmem(channels, width),
        vmem(channels, width),
        vmem(channels, width),
        vmem(channels, width),
        vmem(ny, drows, width),
        vmem(ny, drows, width),
        vmem(ny, drows, width, dtype=F32),
        vmem(4, reach, drows, width // 2),
        vmem(4, reach, drows, width // 2),
        dma(3, nz - 1), dma(3, nz - 1),
        dma(3, nx - 1), dma(3, nx - 1),
        dma(ny), dma(ny),
        dma(4, reach), dma(4, reach),
    ]
    return pl.pallas_call(
        functools.partial(kernel, nz, nx, ny),
        out_shape=jax.ShapeDtypeStruct((drows, width), BF16),
        in_specs=[pl.BlockSpec(memory_space=pltpu.VMEM)] * 11,
        out_specs=pl.BlockSpec(memory_space=pltpu.VMEM),
        scratch_shapes=scratch,
        compiler_params=pltpu.CompilerParams(
            collective_id=0, has_side_effects=True, vmem_limit_bytes=40 << 20
        ),
    )(gate_q, key_k, value_v, filter_taps, skip_bias.reshape(1, channels), w_out, *consts)


def solution(mesh):
    nz, ny = mesh.shape["ctx"] // NX, mesh.shape["tp"] // 2
    return jax.shard_map(
        functools.partial(body, nz, NX, ny),
        mesh=mesh,
        in_specs=(
            P("tp", "ctx"),
            P("tp", "ctx"),
            P("tp", "ctx"),
            P("tp", "ctx"),
            P("tp"),
            P("tp", None),
        ),
        out_specs=P("tp", "ctx"),
        check_vma=False,
    )
```

```python
import functools

import jax
import jax.numpy as jnp
import ml_dtypes
import numpy as np
from jax import lax
from jax.experimental import pallas as pl
from jax.experimental.pallas import tpu as pltpu
from jax.sharding import PartitionSpec as P

MESH = pl.DeviceIdType.MESH
F32 = jnp.float32
BF16 = jnp.bfloat16
NX = 4


def split_np(table):
    high = np.asarray(table, np.float32).astype(ml_dtypes.bfloat16)
    low = (table - high.astype(np.float64)).astype(ml_dtypes.bfloat16)
    return [high, low]


def tables(nz, nx, own, width):
    shards = nz * nx
    length = shards * width
    freq = np.arange(shards) - 0.25
    block = np.array([z * nx + x for x in range(nx) for z in range(nz)])
    first = 2.0 * np.pi * np.outer(freq, block) / shards
    eye = np.eye(own)
    spread = lambda m: np.einsum("ki,cd->ckid", m, eye).reshape(own * shards, shards * own)
    ahead = np.stack(split_np(spread(np.cos(first))) + split_np(spread(-np.sin(first))))
    back = np.stack(
        split_np(spread(np.cos(first)).T / length) + split_np(spread(-np.sin(first)).T / length)
    )
    angle = 2.0 * np.pi * np.outer(freq, np.arange(width)) / length
    twist = np.stack([np.cos(angle), np.sin(angle)]).astype(np.float32)
    angle = 2.0 * np.pi * (np.outer(np.arange(width), np.arange(width)) % width) / width
    inner = np.stack(split_np(np.cos(angle)) + split_np(np.sin(angle)))
    rows = shards * own
    order = np.arange(rows).reshape(nz, nx, own).transpose(1, 0, 2).reshape(-1)
    to_x = np.zeros((rows, rows))
    to_x[np.arange(rows), order] = 1.0
    perm = np.stack([to_x, to_x.T]).astype(ml_dtypes.bfloat16)
    return ahead, back, twist, inner, perm


def dot(a, b):
    return jnp.dot(a, b, preferred_element_type=F32)


def split(a):
    high = a.astype(BF16)
    return high, (a - high.astype(F32)).astype(BF16)


def dot3(a, b):
    return dot(a[0], b[0]) + (dot(a[0], b[1]) + dot(a[1], b[0]))


def kernel(
    nz, nx, ny,
    gate_h, key_h, value_h, taps_h, skip_h, w_h, ahead_h, back_h, twist_h, inner_h, perm_h,
    out,
    gate, key, value, taps, skip, w, ahead, back, twist, inner, perm, in_sem,
    sig, skip_cols, w_t, zsend, zbuf, xsend, xbuf, spec, csend, cbuf, dsend, conv,
    psend, precv, own, rsend, rrecv,
    zs_sem, zr_sem, xs_sem, xr_sem, ps_sem, pr_sem, rs_sem, rr_sem,
):
    channels, width = key.shape
    shards = nz * nx
    mine = channels // shards
    zrows = nx * mine
    xrows = nz * mine
    drows = out.shape[0]
    half = width // 2
    ctx = lax.axis_index("ctx")
    tp = lax.axis_index("tp")
    z, x = ctx // nx, ctx % nx
    y, core = tp // 2, tp % 2

    def z_at(o):
        return (z + o + nz) % nz

    def x_at(o):
        return (x + o) % nx

    def y_at(o):
        return (y + o + ny) % ny

    def z_peer(o):
        return {"ctx": z_at(o) * nx + x}

    def x_peer(o):
        return {"ctx": z * nx + x_at(o)}

    def y_peer(o):
        return {"tp": y_at(o) * 2 + core}

    partner = {"tp": y * 2 + (1 - core)}
    z_order = [nz // 2]
    for o in range(nz // 2 - 1, 0, -1):
        z_order += [o, -o]
    x_order = list(range(1, nx))

    loads = {}
    for n, (name, source, target) in enumerate((
        ("taps", taps_h, taps),
        ("key", key_h, key),
        ("value", value_h, value),
        ("perm", perm_h, perm),
        ("w", w_h, w),
        ("skip", skip_h, skip),
        ("ahead", ahead_h, ahead),
        ("twist", twist_h, twist),
        ("inner", inner_h, inner),
        ("back", back_h, back),
        ("gate", gate_h, gate),
    )):
        loads[name] = pltpu.make_async_copy(source, target, in_sem.at[n])
        loads[name].start()

    def loaded(*names):
        for name in names:
            loads[name].wait()

    barrier = pltpu.get_barrier_semaphore()
    peers = [z_peer(o) for o in z_order] + [x_peer(o) for o in x_order]
    peers += [partner, y_peer(1), y_peer(-1)]
    for peer in peers:
        pl.semaphore_signal(barrier, inc=1, device_id=peer, device_id_type=MESH)

    started = []

    def rows_z(i):
        return pl.ds(pl.multiple_of(i * zrows, zrows), zrows)

    def rows_x(i):
        return pl.ds(pl.multiple_of(i * xrows, xrows), xrows)

    def z_copy(kind, source, target, n, o):
        return pltpu.make_async_remote_copy(
            src_ref=source.at[rows_z(z_at(o))],
            dst_ref=target.at[rows_z(z)],
            send_sem=zs_sem.at[kind, n],
            recv_sem=zr_sem.at[kind, n],
            device_id=z_peer(o),
            device_id_type=MESH,
        )

    def x_copy(kind, source, target, n, o):
        return pltpu.make_async_remote_copy(
            src_ref=source.at[rows_x(x_at(o))],
            dst_ref=target.at[rows_x(x)],
            send_sem=xs_sem.at[kind, n],
            recv_sem=xr_sem.at[kind, n],
            device_id=x_peer(o),
            device_id_type=MESH,
        )

    far = len(z_order) // 2

    def z_copies(kind, source, target):
        copies = [z_copy(kind, source, target, n, o) for n, o in enumerate(z_order)]
        started.extend(copies)
        return copies

    def z_start(copies):
        for copy in copies:
            copy.start()

    def z_keep(source, target):
        target[rows_z(z), :] = source[rows_z(z), :]

    def x_start(kind, source, target):
        copies = [x_copy(kind, source, target, n, o) for n, o in enumerate(x_order)]
        for copy in copies:
            copy.start()
        target[rows_x(x), :] = source[rows_x(x), :]
        started.extend(copies)
        return copies

    def arrive(copies):
        for copy in copies:
            copy.wait_recv()

    tall = lambda t: jnp.concatenate([t] * mine, axis=0)

    def forward(rows):
        re = dot(ahead[0], rows) + dot(ahead[1], rows)
        im = dot(ahead[2], rows) + dot(ahead[3], rows)
        cos_t, sin_t = tall(twist[0]), tall(twist[1])
        mid_re, mid_im = split(re * cos_t + im * sin_t), split(im * cos_t - re * sin_t)
        cos_p, sin_p = (inner[0], inner[1]), (inner[2], inner[3])
        return (
            dot3(mid_re, cos_p) + dot3(mid_im, sin_p),
            dot3(mid_im, cos_p) - dot3(mid_re, sin_p),
        )

    loaded("taps")
    zsend[0] = taps[...].astype(BF16)
    loaded("key", "value")
    sig[...] = key[...].astype(F32) * value[...].astype(F32)
    zsend[1] = sig[...].astype(BF16)
    taps_z = z_copies(0, zsend.at[0], zbuf.at[0])
    sig_z = z_copies(1, zsend.at[1], zbuf.at[1])
    pl.semaphore_wait(barrier, len(peers))
    z_start(taps_z[:far])
    z_start(sig_z[:far])
    z_start(taps_z[far:])
    z_start(sig_z[far:])
    z_keep(zsend.at[0], zbuf.at[0])
    z_keep(zsend.at[1], zbuf.at[1])

    loaded("skip", "w")
    skip_cols[...] = jnp.broadcast_to(skip[...], (width, channels)).T
    for j in range(w.shape[1] // drows):
        w_t[pl.ds(j * drows, drows), :] = w[:, pl.ds(j * drows, drows)].T

    loaded("perm")
    arrive(taps_z)
    xsend[0] = dot(perm[0], zbuf[0]).astype(BF16)
    taps_x = x_start(0, xsend.at[0], xbuf.at[0])
    arrive(sig_z)
    xsend[1] = dot(perm[0], zbuf[1]).astype(BF16)
    sig_x = x_start(1, xsend.at[1], xbuf.at[1])
    loaded("ahead", "twist", "inner")
    arrive(taps_x)
    spec_re, spec_im = forward(xbuf[0])
    spec[0] = spec_re
    spec[1] = spec_im
    arrive(sig_x)

    sre, sim = forward(xbuf[1])
    tre, tim = spec[0], spec[1]
    pre, pim = split(sre * tre - sim * tim), split(sre * tim + sim * tre)
    cos_p, sin_p = (inner[0], inner[1]), (inner[2], inner[3])
    re = dot3(pre, cos_p) - dot3(pim, sin_p)
    im = dot3(pim, cos_p) + dot3(pre, sin_p)
    cos_t, sin_t = tall(twist[0]), tall(twist[1])
    re, im = split(re * cos_t - im * sin_t), split(im * cos_t + re * sin_t)
    loaded("back")
    csend[...] = (dot3((back[0], back[1]), re) + dot3((back[2], back[3]), im)).astype(BF16)

    conv_x = x_start(2, csend, cbuf)
    arrive(conv_x)
    dsend[...] = dot(perm[1], cbuf[...]).astype(BF16)
    conv_z = z_copies(2, dsend, conv)
    z_start(conv_z)
    z_keep(dsend, conv)
    loaded("gate")
    arrive(conv_z)

    gated = (
        gate[...].astype(F32) * (conv[...].astype(F32) + skip_cols[...] * sig[...])
    ).astype(BF16)

    reach = ny // 2
    offsets = [reach]
    for o in range(reach - 1, 0, -1):
        offsets += [o, -o]
    offsets += [0]
    slot = {o: n for n, o in enumerate(offsets)}
    slot[-reach] = 0

    def weight_rows(o, side):
        return w_t[pl.ds(pl.multiple_of((y_at(o) * 2 + side) * drows, drows), drows), :]

    pair = []
    for n, o in enumerate(offsets):
        psend[n] = dot(weight_rows(o, 1 - core), gated).astype(BF16)
        copy = pltpu.make_async_remote_copy(
            src_ref=psend.at[n],
            dst_ref=precv.at[n],
            send_sem=ps_sem.at[n],
            recv_sem=pr_sem.at[n],
            device_id=partner,
            device_id_type=MESH,
        )
        copy.start()
        pair.append(copy)
        own[n] = dot(weight_rows(o, core), gated)
    started.extend(pair)

    there = set()

    def chip_sum(o, lanes):
        n = slot[o]
        if n not in there:
            pair[n].wait_recv()
            there.add(n)
        return own[n, :, lanes] + precv[n, :, lanes].astype(F32)

    low, high = pl.ds(0, half), pl.ds(half, half)
    rings = [(1, low, reach), (-1, high, reach), (1, high, reach - 1), (-1, low, reach - 1)]
    last = [None] * len(rings)
    for step in range(reach):
        for r, (way, lanes, begin) in enumerate(rings):
            distance = begin - step
            if distance < 1:
                continue
            total = chip_sum(way * distance, lanes)
            if last[r] is not None:
                last[r].wait_recv()
                total = total + rrecv[r, step - 1].astype(F32)
            rsend[r, step] = total.astype(BF16)
            copy = pltpu.make_async_remote_copy(
                src_ref=rsend.at[r, step],
                dst_ref=rrecv.at[r, step],
                send_sem=rs_sem.at[r, step],
                recv_sem=rr_sem.at[r, step],
                device_id=y_peer(way),
                device_id_type=MESH,
            )
            copy.start()
            started.append(copy)
            last[r] = copy
    for lanes, ends in ((low, (0, 3)), (high, (1, 2))):
        total = chip_sum(0, lanes)
        for r in ends:
            if last[r] is not None:
                last[r].wait_recv()
                total = total + rrecv[r, rings[r][2] - 1].astype(F32)
        out[:, lanes] = total.astype(BF16)

    for copy in started:
        copy.wait_send()


def body(nz, nx, ny, gate_q, key_k, value_v, filter_taps, skip_bias, w_out):
    channels, width = key_k.shape
    depth = w_out.shape[1]
    drows = depth // (2 * ny)
    reach = ny // 2
    consts = tables(nz, nx, channels // (nz * nx), width)
    vmem = lambda *shape, dtype=BF16: pltpu.VMEM(shape, dtype)
    dma = lambda *shape: pltpu.SemaphoreType.DMA(shape)
    operands = (
        gate_q, key_k, value_v, filter_taps, skip_bias.reshape(1, channels), w_out, *consts
    )
    scratch = [vmem(*a.shape, dtype=a.dtype) for a in operands]
    scratch += [
        dma(len(operands)),
        vmem(channels, width, dtype=F32),
        vmem(channels, width, dtype=F32),
        vmem(depth, channels),
        vmem(2, channels, width),
        vmem(2, channels, width),
        vmem(2, channels, width),
        vmem(2, channels, width),
        vmem(2, channels, width, dtype=F32),
        vmem(channels, width),
        vmem(channels, width),
        vmem(channels, width),
        vmem(channels, width),
        vmem(ny, drows, width),
        vmem(ny, drows, width),
        vmem(ny, drows, width, dtype=F32),
        vmem(4, reach, drows, width // 2),
        vmem(4, reach, drows, width // 2),
        dma(3, nz - 1), dma(3, nz - 1),
        dma(3, nx - 1), dma(3, nx - 1),
        dma(ny), dma(ny),
        dma(4, reach), dma(4, reach),
    ]
    return pl.pallas_call(
        functools.partial(kernel, nz, nx, ny),
        out_shape=jax.ShapeDtypeStruct((drows, width), BF16),
        in_specs=[pl.BlockSpec(memory_space=pltpu.HBM)] * len(operands),
        out_specs=pl.BlockSpec(memory_space=pltpu.VMEM),
        scratch_shapes=scratch,
        compiler_params=pltpu.CompilerParams(
            collective_id=0, has_side_effects=True, vmem_limit_bytes=60 << 20
        ),
    )(*operands)


def solution(mesh):
    nz, ny = mesh.shape["ctx"] // NX, mesh.shape["tp"] // 2
    return jax.shard_map(
        functools.partial(body, nz, NX, ny),
        mesh=mesh,
        in_specs=(
            P("tp", "ctx"),
            P("tp", "ctx"),
            P("tp", "ctx"),
            P("tp", "ctx"),
            P("tp"),
            P("tp", None),
        ),
        out_specs=P("tp", "ctx"),
        check_vma=False,
    )
```

```python
import functools

import jax
import jax.numpy as jnp
import ml_dtypes
import numpy as np
from jax import lax
from jax.experimental import pallas as pl
from jax.experimental.pallas import tpu as pltpu
from jax.sharding import PartitionSpec as P

MESH = pl.DeviceIdType.MESH
F32 = jnp.float32
BF16 = jnp.bfloat16
ROW_PARTS = 2
NX = 4


def split_np(table):
    high = np.asarray(table, np.float32).astype(ml_dtypes.bfloat16)
    low = (table - high.astype(np.float64)).astype(ml_dtypes.bfloat16)
    return [high, low]


def tables(nz, nx, own, width):
    shards = nz * nx
    length = shards * width
    freq = np.arange(shards) - 0.25
    block = np.array([z * nx + x for x in range(nx) for z in range(nz)])
    first = 2.0 * np.pi * np.outer(freq, block) / shards
    eye = np.eye(own)
    spread = lambda m: np.einsum("ki,cd->ckid", m, eye).reshape(own * shards, shards * own)
    ahead = np.stack(split_np(spread(np.cos(first))) + split_np(spread(-np.sin(first))))
    back = np.stack(
        split_np(spread(np.cos(first)).T / length) + split_np(spread(-np.sin(first)).T / length)
    )
    angle = 2.0 * np.pi * np.outer(freq, np.arange(width)) / length
    twist = np.stack([np.cos(angle), np.sin(angle)]).astype(np.float32)
    angle = 2.0 * np.pi * (np.outer(np.arange(width), np.arange(width)) % width) / width
    inner = np.stack(split_np(np.cos(angle)) + split_np(np.sin(angle)))
    rows = shards * own
    order = np.arange(rows).reshape(nz, nx, own).transpose(1, 0, 2).reshape(-1)
    to_x = np.zeros((rows, rows))
    to_x[np.arange(rows), order] = 1.0
    perm = np.stack([to_x, to_x.T]).astype(ml_dtypes.bfloat16)
    return ahead, back, twist, inner, perm


def dot(a, b):
    return jnp.dot(a, b, preferred_element_type=F32)


def split(a):
    high = a.astype(BF16)
    return high, (a - high.astype(F32)).astype(BF16)


def dot3(a, b):
    return dot(a[0], b[0]) + (dot(a[0], b[1]) + dot(a[1], b[0]))


def kernel(
    nz, nx, ny,
    gate_h, key_h, value_h, taps_h, skip_h, w_h, ahead_h, back_h, twist_h, inner_h, perm_h,
    out,
    gate, key, value, taps, skip, w, ahead, back, twist, inner, perm, in_sem,
    sig, skip_cols, w_t, zsend, zbuf, xsend, xbuf, spec, csend, cbuf, dsend, conv,
    psend, precv, own, rsend, rrecv,
    zs_sem, zr_sem, xs_sem, xr_sem, ps_sem, pr_sem, rs_sem, rr_sem,
):
    channels, width = key.shape
    shards = nz * nx
    mine = channels // shards
    zrows = nx * mine
    xrows = nz * mine
    drows = out.shape[0]
    half = width // 2
    ctx = lax.axis_index("ctx")
    tp = lax.axis_index("tp")
    z, x = ctx // nx, ctx % nx
    y, core = tp // 2, tp % 2

    def z_at(o):
        return (z + o + nz) % nz

    def x_at(o):
        return (x + o) % nx

    def y_at(o):
        return (y + o + ny) % ny

    def z_peer(o):
        return {"ctx": z_at(o) * nx + x}

    def x_peer(o):
        return {"ctx": z * nx + x_at(o)}

    def y_peer(o):
        return {"tp": y_at(o) * 2 + core}

    partner = {"tp": y * 2 + (1 - core)}
    z_order = [nz // 2]
    for o in range(nz // 2 - 1, 0, -1):
        z_order += [o, -o]
    x_order = list(range(1, nx))

    barrier = pltpu.get_barrier_semaphore()
    peers = [z_peer(o) for o in z_order] + [x_peer(o) for o in x_order]
    peers += [partner, y_peer(1), y_peer(-1)]
    for peer in peers:
        pl.semaphore_signal(barrier, inc=1, device_id=peer, device_id_type=MESH)

    loads = {}
    for n, (name, source, target) in enumerate((
        ("taps", taps_h, taps),
        ("key", key_h, key),
        ("value", value_h, value),
        ("perm", perm_h, perm),
        ("w", w_h, w),
        ("skip", skip_h, skip),
        ("ahead", ahead_h, ahead),
        ("twist", twist_h, twist),
        ("inner", inner_h, inner),
        ("back", back_h, back),
        ("gate", gate_h, gate),
    )):
        loads[name] = pltpu.make_async_copy(source, target, in_sem.at[n])
        loads[name].start()

    def loaded(*names):
        for name in names:
            loads[name].wait()

    started = []

    def rows_z(i):
        return pl.ds(pl.multiple_of(i * zrows, zrows), zrows)

    def rows_x(i):
        return pl.ds(pl.multiple_of(i * xrows, xrows), xrows)

    def z_copy(kind, source, target, n, o):
        return pltpu.make_async_remote_copy(
            src_ref=source.at[rows_z(z_at(o))],
            dst_ref=target.at[rows_z(z)],
            send_sem=zs_sem.at[kind, n],
            recv_sem=zr_sem.at[kind, n],
            device_id=z_peer(o),
            device_id_type=MESH,
        )

    def x_copy(kind, source, target, n, o):
        return pltpu.make_async_remote_copy(
            src_ref=source.at[rows_x(x_at(o))],
            dst_ref=target.at[rows_x(x)],
            send_sem=xs_sem.at[kind, n],
            recv_sem=xr_sem.at[kind, n],
            device_id=x_peer(o),
            device_id_type=MESH,
        )

    far = len(z_order) // 2

    def z_copies(kind, source, target):
        copies = [z_copy(kind, source, target, n, o) for n, o in enumerate(z_order)]
        started.extend(copies)
        return copies

    def z_start(copies):
        for copy in copies:
            copy.start()

    def z_keep(source, target):
        target[rows_z(z), :] = source[rows_z(z), :]

    def x_start(kind, source, target):
        copies = [x_copy(kind, source, target, n, o) for n, o in enumerate(x_order)]
        for copy in copies:
            copy.start()
        target[rows_x(x), :] = source[rows_x(x), :]
        started.extend(copies)
        return copies

    def arrive(copies):
        for copy in copies:
            copy.wait_recv()

    tall = lambda t: jnp.concatenate([t] * mine, axis=0)

    def forward(rows):
        re = dot(ahead[0], rows) + dot(ahead[1], rows)
        im = dot(ahead[2], rows) + dot(ahead[3], rows)
        cos_t, sin_t = tall(twist[0]), tall(twist[1])
        mid_re, mid_im = split(re * cos_t + im * sin_t), split(im * cos_t - re * sin_t)
        cos_p, sin_p = (inner[0], inner[1]), (inner[2], inner[3])
        return (
            dot3(mid_re, cos_p) + dot3(mid_im, sin_p),
            dot3(mid_im, cos_p) - dot3(mid_re, sin_p),
        )

    loaded("taps")
    zsend[0] = taps[...].astype(BF16)
    loaded("key", "value")
    sig[...] = key[...].astype(F32) * value[...].astype(F32)
    zsend[1] = sig[...].astype(BF16)
    taps_z = z_copies(0, zsend.at[0], zbuf.at[0])
    sig_z = z_copies(1, zsend.at[1], zbuf.at[1])
    pl.semaphore_wait(barrier, len(peers))
    z_start(taps_z[:far])
    z_start(sig_z[:far])
    z_start(taps_z[far:])
    z_start(sig_z[far:])
    z_keep(zsend.at[0], zbuf.at[0])
    z_keep(zsend.at[1], zbuf.at[1])

    loaded("skip", "w")
    skip_cols[...] = jnp.broadcast_to(skip[...], (width, channels)).T
    for j in range(w.shape[1] // drows):
        w_t[pl.ds(j * drows, drows), :] = w[:, pl.ds(j * drows, drows)].T

    loaded("perm")
    arrive(taps_z)
    xsend[0] = dot(perm[0], zbuf[0]).astype(BF16)
    taps_x = x_start(0, xsend.at[0], xbuf.at[0])
    arrive(sig_z)
    xsend[1] = dot(perm[0], zbuf[1]).astype(BF16)
    sig_x = x_start(1, xsend.at[1], xbuf.at[1])
    loaded("ahead", "twist", "inner")
    arrive(taps_x)
    spec_re, spec_im = forward(xbuf[0])
    spec[0] = spec_re
    spec[1] = spec_im
    arrive(sig_x)

    sre, sim = forward(xbuf[1])
    tre, tim = spec[0], spec[1]
    pre, pim = split(sre * tre - sim * tim), split(sre * tim + sim * tre)
    cos_p, sin_p = (inner[0], inner[1]), (inner[2], inner[3])
    re = dot3(pre, cos_p) - dot3(pim, sin_p)
    im = dot3(pim, cos_p) + dot3(pre, sin_p)
    cos_t, sin_t = tall(twist[0]), tall(twist[1])
    re, im = split(re * cos_t - im * sin_t), split(im * cos_t + re * sin_t)
    loaded("back")
    csend[...] = (dot3((back[0], back[1]), re) + dot3((back[2], back[3]), im)).astype(BF16)

    conv_x = x_start(2, csend, cbuf)
    arrive(conv_x)
    dsend[...] = dot(perm[1], cbuf[...]).astype(BF16)
    conv_z = z_copies(2, dsend, conv)
    z_start(conv_z)
    z_keep(dsend, conv)
    loaded("gate")
    arrive(conv_z)

    gated = (
        gate[...].astype(F32) * (conv[...].astype(F32) + skip_cols[...] * sig[...])
    ).astype(BF16)

    reach = ny // 2
    offsets = [reach]
    for o in range(reach - 1, 0, -1):
        offsets += [o, -o]
    offsets += [0]
    slot = {o: n for n, o in enumerate(offsets)}
    slot[-reach] = 0

    def weight_rows(o, side):
        return w_t[pl.ds(pl.multiple_of((y_at(o) * 2 + side) * drows, drows), drows), :]

    pair = {}

    def send_pair(n):
        psend[n] = dot(weight_rows(offsets[n], 1 - core), gated).astype(BF16)
        pair[n] = pltpu.make_async_remote_copy(
            src_ref=psend.at[n],
            dst_ref=precv.at[n],
            send_sem=ps_sem.at[n],
            recv_sem=pr_sem.at[n],
            device_id=partner,
            device_id_type=MESH,
        )
        pair[n].start()
        started.append(pair[n])

    def keep_own(n):
        own[n] = dot(weight_rows(offsets[n], core), gated)

    there = set()

    def chip_sum(o, rows, lanes):
        n = slot[o]
        if n not in there:
            pair[n].wait_recv()
            there.add(n)
        return own[n, rows, lanes] + precv[n, rows, lanes].astype(F32)

    low, high = pl.ds(0, half), pl.ds(half, half)
    parts = drows // ROW_PARTS
    pieces = [pl.ds(k * parts, parts) for k in range(ROW_PARTS)]
    rings = []
    for begin in (reach, reach - 1):
        for rows in pieces:
            rings += [(1, rows, low if begin == reach else high, begin)]
            rings += [(-1, rows, high if begin == reach else low, begin)]
    last = [None] * len(rings)

    def ring_step(step):
        for r, (way, rows, lanes, begin) in enumerate(rings):
            distance = begin - step
            if distance < 1:
                continue
            total = chip_sum(way * distance, rows, lanes)
            if last[r] is not None:
                last[r].wait_recv()
                total = total + rrecv[r, step - 1].astype(F32)
            rsend[r, step] = total.astype(BF16)
            copy = pltpu.make_async_remote_copy(
                src_ref=rsend.at[r, step],
                dst_ref=rrecv.at[r, step],
                send_sem=rs_sem.at[r, step],
                recv_sem=rr_sem.at[r, step],
                device_id=y_peer(way),
                device_id_type=MESH,
            )
            copy.start()
            started.append(copy)
            last[r] = copy

    for n in range(ny):
        send_pair(n)
    for n in range(ny):
        keep_own(n)
    for step in range(reach):
        ring_step(step)
    for rows in pieces:
        for lanes in (low, high):
            total = chip_sum(0, rows, lanes)
            for r, ring in enumerate(rings):
                if ring[1] is rows and ring[2] is lanes and last[r] is not None:
                    last[r].wait_recv()
                    total = total + rrecv[r, ring[3] - 1].astype(F32)
            out[rows, lanes] = total.astype(BF16)

    for copy in started:
        copy.wait_send()


def body(nz, nx, ny, gate_q, key_k, value_v, filter_taps, skip_bias, w_out):
    channels, width = key_k.shape
    depth = w_out.shape[1]
    drows = depth // (2 * ny)
    reach = ny // 2
    consts = tables(nz, nx, channels // (nz * nx), width)
    vmem = lambda *shape, dtype=BF16: pltpu.VMEM(shape, dtype)
    dma = lambda *shape: pltpu.SemaphoreType.DMA(shape)
    operands = (
        gate_q, key_k, value_v, filter_taps, skip_bias.reshape(1, channels), w_out, *consts
    )
    scratch = [vmem(*a.shape, dtype=a.dtype) for a in operands]
    scratch += [
        dma(len(operands)),
        vmem(channels, width, dtype=F32),
        vmem(channels, width, dtype=F32),
        vmem(depth, channels),
        vmem(2, channels, width),
        vmem(2, channels, width),
        vmem(2, channels, width),
        vmem(2, channels, width),
        vmem(2, channels, width, dtype=F32),
        vmem(channels, width),
        vmem(channels, width),
        vmem(channels, width),
        vmem(channels, width),
        vmem(ny, drows, width),
        vmem(ny, drows, width),
        vmem(ny, drows, width, dtype=F32),
        vmem(4 * ROW_PARTS, reach, drows // ROW_PARTS, width // 2),
        vmem(4 * ROW_PARTS, reach, drows // ROW_PARTS, width // 2),
        dma(3, nz - 1), dma(3, nz - 1),
        dma(3, nx - 1), dma(3, nx - 1),
        dma(ny), dma(ny),
        dma(4 * ROW_PARTS, reach), dma(4 * ROW_PARTS, reach),
    ]
    return pl.pallas_call(
        functools.partial(kernel, nz, nx, ny),
        out_shape=jax.ShapeDtypeStruct((drows, width), BF16),
        in_specs=[pl.BlockSpec(memory_space=pltpu.HBM)] * len(operands),
        out_specs=pl.BlockSpec(memory_space=pltpu.VMEM),
        scratch_shapes=scratch,
        compiler_params=pltpu.CompilerParams(
            collective_id=0, has_side_effects=True, vmem_limit_bytes=40 << 20
        ),
    )(*[pltpu.with_memory_space_constraint(a, pltpu.HBM) for a in operands])


def solution(mesh):
    nz, ny = mesh.shape["ctx"] // NX, mesh.shape["tp"] // 2
    return jax.shard_map(
        functools.partial(body, nz, NX, ny),
        mesh=mesh,
        in_specs=(
            P("tp", "ctx"),
            P("tp", "ctx"),
            P("tp", "ctx"),
            P("tp", "ctx"),
            P("tp"),
            P("tp", None),
        ),
        out_specs=P("tp", "ctx"),
        check_vma=False,
    )
```

```python
import functools

import jax
import jax.numpy as jnp
import ml_dtypes
import numpy as np
from jax import lax
from jax.experimental import pallas as pl
from jax.experimental.pallas import tpu as pltpu
from jax.sharding import PartitionSpec as P

MESH = pl.DeviceIdType.MESH
F32 = jnp.float32
BF16 = jnp.bfloat16
ROW_PARTS = 4
OFFSETS = (4, 3, -3, 2, -2, 1, -1, 0)
NX = 4


def split_np(table):
    high = np.asarray(table, np.float32).astype(ml_dtypes.bfloat16)
    low = (table - high.astype(np.float64)).astype(ml_dtypes.bfloat16)
    return [high, low]


def tables(nz, nx, own, width):
    shards = nz * nx
    length = shards * width
    freq = np.arange(shards) - 0.25
    block = np.array([z * nx + x for x in range(nx) for z in range(nz)])
    first = 2.0 * np.pi * np.outer(freq, block) / shards
    eye = np.eye(own)
    spread = lambda m: np.einsum("ki,cd->ckid", m, eye).reshape(own * shards, shards * own)
    ahead = np.stack(split_np(spread(np.cos(first))) + split_np(spread(-np.sin(first))))
    back = np.stack(
        split_np(spread(np.cos(first)).T / length) + split_np(spread(-np.sin(first)).T / length)
    )
    angle = 2.0 * np.pi * np.outer(freq, np.arange(width)) / length
    twist = np.stack([np.cos(angle), np.sin(angle)]).astype(np.float32)
    angle = 2.0 * np.pi * (np.outer(np.arange(width), np.arange(width)) % width) / width
    inner = np.stack(split_np(np.cos(angle)) + split_np(np.sin(angle)))
    rows = shards * own
    order = np.arange(rows).reshape(nz, nx, own).transpose(1, 0, 2).reshape(-1)
    to_x = np.zeros((rows, rows))
    to_x[np.arange(rows), order] = 1.0
    perm = np.stack([to_x, to_x.T]).astype(ml_dtypes.bfloat16)
    return ahead, back, twist, inner, perm


def dot(a, b):
    return jnp.dot(a, b, preferred_element_type=F32)


def split(a):
    high = a.astype(BF16)
    return high, (a - high.astype(F32)).astype(BF16)


def dot3(a, b):
    return dot(a[0], b[0]) + (dot(a[0], b[1]) + dot(a[1], b[0]))


def kernel(
    nz, nx, ny,
    gate_h, key_h, value_h, taps_h, skip_h, w_h, ahead_h, back_h, twist_h, inner_h, perm_h,
    out,
    gate, key, value, taps, skip, w, ahead, back, twist, inner, perm, in_sem,
    sig, skip_cols, w_t, zsend, zbuf, xsend, xbuf, spec, csend, cbuf, dsend, conv,
    psend, precv, own, rsend, rrecv,
    zs_sem, zr_sem, xs_sem, xr_sem, ps_sem, pr_sem, rs_sem, rr_sem,
):
    channels, width = key.shape
    shards = nz * nx
    mine = channels // shards
    zrows = nx * mine
    xrows = nz * mine
    drows = out.shape[0]
    half = width // 2
    ctx = lax.axis_index("ctx")
    tp = lax.axis_index("tp")
    z, x = ctx // nx, ctx % nx
    y, core = tp // 2, tp % 2

    def z_at(o):
        return (z + o + nz) % nz

    def x_at(o):
        return (x + o) % nx

    def y_at(o):
        return (y + o + ny) % ny

    def z_peer(o):
        return {"ctx": z_at(o) * nx + x}

    def x_peer(o):
        return {"ctx": z * nx + x_at(o)}

    def y_peer(o):
        return {"tp": y_at(o) * 2 + core}

    partner = {"tp": y * 2 + (1 - core)}
    z_order = [nz // 2]
    for o in range(nz // 2 - 1, 0, -1):
        z_order += [o, -o]
    x_order = list(range(1, nx))

    barrier = pltpu.get_barrier_semaphore()
    peers = [z_peer(o) for o in z_order] + [x_peer(o) for o in x_order]
    peers += [partner, y_peer(1), y_peer(-1), y_peer(2), y_peer(-2)]
    for peer in peers:
        pl.semaphore_signal(barrier, inc=1, device_id=peer, device_id_type=MESH)

    loads = {}
    for n, (name, source, target) in enumerate((
        ("taps", taps_h, taps),
        ("key", key_h, key),
        ("value", value_h, value),
        ("perm", perm_h, perm),
        ("w", w_h, w),
        ("skip", skip_h, skip),
        ("ahead", ahead_h, ahead),
        ("twist", twist_h, twist),
        ("inner", inner_h, inner),
        ("back", back_h, back),
        ("gate", gate_h, gate),
    )):
        loads[name] = pltpu.make_async_copy(source, target, in_sem.at[n])
        loads[name].start()

    def loaded(*names):
        for name in names:
            loads[name].wait()

    started = []

    def rows_z(i):
        return pl.ds(pl.multiple_of(i * zrows, zrows), zrows)

    def rows_x(i):
        return pl.ds(pl.multiple_of(i * xrows, xrows), xrows)

    def z_copy(kind, source, target, n, o):
        return pltpu.make_async_remote_copy(
            src_ref=source.at[rows_z(z_at(o))],
            dst_ref=target.at[rows_z(z)],
            send_sem=zs_sem.at[kind, n],
            recv_sem=zr_sem.at[kind, n],
            device_id=z_peer(o),
            device_id_type=MESH,
        )

    def x_copy(kind, source, target, n, o):
        return pltpu.make_async_remote_copy(
            src_ref=source.at[rows_x(x_at(o))],
            dst_ref=target.at[rows_x(x)],
            send_sem=xs_sem.at[kind, n],
            recv_sem=xr_sem.at[kind, n],
            device_id=x_peer(o),
            device_id_type=MESH,
        )

    far = len(z_order) // 2

    def z_copies(kind, source, target):
        copies = [z_copy(kind, source, target, n, o) for n, o in enumerate(z_order)]
        started.extend(copies)
        return copies

    def z_start(copies):
        for copy in copies:
            copy.start()

    def z_keep(source, target):
        target[rows_z(z), :] = source[rows_z(z), :]

    def x_start(kind, source, target):
        copies = [x_copy(kind, source, target, n, o) for n, o in enumerate(x_order)]
        for copy in copies:
            copy.start()
        target[rows_x(x), :] = source[rows_x(x), :]
        started.extend(copies)
        return copies

    def arrive(copies):
        for copy in copies:
            copy.wait_recv()

    tall = lambda t: jnp.concatenate([t] * mine, axis=0)

    def forward(rows):
        re = dot(ahead[0], rows) + dot(ahead[1], rows)
        im = dot(ahead[2], rows) + dot(ahead[3], rows)
        cos_t, sin_t = tall(twist[0]), tall(twist[1])
        mid_re, mid_im = split(re * cos_t + im * sin_t), split(im * cos_t - re * sin_t)
        cos_p, sin_p = (inner[0], inner[1]), (inner[2], inner[3])
        return (
            dot3(mid_re, cos_p) + dot3(mid_im, sin_p),
            dot3(mid_im, cos_p) - dot3(mid_re, sin_p),
        )

    loaded("taps")
    zsend[0] = taps[...].astype(BF16)
    loaded("key", "value")
    sig[...] = key[...].astype(F32) * value[...].astype(F32)
    zsend[1] = sig[...].astype(BF16)
    taps_z = z_copies(0, zsend.at[0], zbuf.at[0])
    sig_z = z_copies(1, zsend.at[1], zbuf.at[1])
    pl.semaphore_wait(barrier, len(peers))
    z_start(taps_z[:far])
    z_start(sig_z[:far])
    z_start(taps_z[far:])
    z_start(sig_z[far:])
    z_keep(zsend.at[0], zbuf.at[0])
    z_keep(zsend.at[1], zbuf.at[1])

    loaded("skip", "w")
    skip_cols[...] = jnp.broadcast_to(skip[...], (width, channels)).T
    for j in range(w.shape[1] // drows):
        w_t[pl.ds(j * drows, drows), :] = w[:, pl.ds(j * drows, drows)].T

    loaded("perm")
    arrive(taps_z)
    xsend[0] = dot(perm[0], zbuf[0]).astype(BF16)
    taps_x = x_start(0, xsend.at[0], xbuf.at[0])
    arrive(sig_z)
    xsend[1] = dot(perm[0], zbuf[1]).astype(BF16)
    sig_x = x_start(1, xsend.at[1], xbuf.at[1])
    loaded("ahead", "twist", "inner")
    arrive(taps_x)
    spec_re, spec_im = forward(xbuf[0])
    spec[0] = spec_re
    spec[1] = spec_im
    arrive(sig_x)

    sre, sim = forward(xbuf[1])
    tre, tim = spec[0], spec[1]
    pre, pim = split(sre * tre - sim * tim), split(sre * tim + sim * tre)
    cos_p, sin_p = (inner[0], inner[1]), (inner[2], inner[3])
    re = dot3(pre, cos_p) - dot3(pim, sin_p)
    im = dot3(pim, cos_p) + dot3(pre, sin_p)
    cos_t, sin_t = tall(twist[0]), tall(twist[1])
    re, im = split(re * cos_t - im * sin_t), split(im * cos_t + re * sin_t)
    loaded("back")
    csend[...] = (dot3((back[0], back[1]), re) + dot3((back[2], back[3]), im)).astype(BF16)

    conv_x = x_start(2, csend, cbuf)
    arrive(conv_x)
    dsend[...] = dot(perm[1], cbuf[...]).astype(BF16)
    conv_z = z_copies(2, dsend, conv)
    z_start(conv_z)
    z_keep(dsend, conv)
    loaded("gate")
    arrive(conv_z)

    gated = (
        gate[...].astype(F32) * (conv[...].astype(F32) + skip_cols[...] * sig[...])
    ).astype(BF16)

    slot = {o: n for n, o in enumerate(OFFSETS)}
    slot[-4] = slot[4]

    def weight_rows(o, side):
        return w_t[pl.ds(pl.multiple_of((y_at(o) * 2 + side) * drows, drows), drows), :]

    pair = {}

    def send_pair(n):
        psend[n] = dot(weight_rows(OFFSETS[n], 1 - core), gated).astype(BF16)
        pair[n] = pltpu.make_async_remote_copy(
            src_ref=psend.at[n],
            dst_ref=precv.at[n],
            send_sem=ps_sem.at[n],
            recv_sem=pr_sem.at[n],
            device_id=partner,
            device_id_type=MESH,
        )
        pair[n].start()
        started.append(pair[n])

    def keep_own(n):
        own[n] = dot(weight_rows(OFFSETS[n], core), gated)

    there = set()

    def chip_sum(o, rows, lanes):
        n = slot[o]
        if n not in there:
            pair[n].wait_recv()
            there.add(n)
        return own[n, rows, lanes] + precv[n, rows, lanes].astype(F32)

    low, high, every = pl.ds(0, half), pl.ds(half, half), pl.ds(0, width)
    ways = ((0, 1, low), (1, -1, high))
    parts = drows // ROW_PARTS
    pieces = [(k, pl.ds(k * parts, parts)) for k in range(ROW_PARTS)]
    hops = {}

    def hop(way, role, piece, lanes, target):
        k, rows = piece
        copy = pltpu.make_async_remote_copy(
            src_ref=rsend.at[way, role, rows, lanes],
            dst_ref=rrecv.at[way, role, rows, lanes],
            send_sem=rs_sem.at[way, role, k],
            recv_sem=rr_sem.at[way, role, k],
            device_id=y_peer(target),
            device_id_type=MESH,
        )
        copy.start()
        started.append(copy)
        hops[way, role, k] = copy

    def came(way, role, piece, lanes):
        return rrecv[way, role, piece[1], lanes].astype(F32)

    for n in range(8):
        send_pair(n)
    for n in range(8):
        keep_own(n)
    for piece in pieces:
        for way, sign, lanes in ways:
            rsend[way, 3, piece[1], lanes] = chip_sum(4 * sign, piece[1], lanes).astype(BF16)
            hop(way, 3, piece, lanes, 2 * sign)
        for way, sign, _ in ways:
            rsend[way, 2, piece[1], :] = chip_sum(3 * sign, piece[1], every).astype(BF16)
            hop(way, 2, piece, every, sign)
    for piece in pieces:
        for way, sign, extra in ways:
            hops[way, 3, piece[0]].wait_recv()
            hops[way, 2, piece[0]].wait_recv()
            for lanes in (low, high):
                total = chip_sum(2 * sign, piece[1], lanes) + came(way, 2, piece, lanes)
                if lanes is extra:
                    total = total + came(way, 3, piece, lanes)
                rsend[way, 1, piece[1], lanes] = total.astype(BF16)
            hop(way, 1, piece, every, sign)
    for piece in pieces:
        for way, sign, _ in ways:
            hops[way, 1, piece[0]].wait_recv()
            total = chip_sum(sign, piece[1], every) + came(way, 1, piece, every)
            rsend[way, 0, piece[1], :] = total.astype(BF16)
            hop(way, 0, piece, every, sign)
    for piece in pieces:
        total = chip_sum(0, piece[1], every)
        for way in (0, 1):
            hops[way, 0, piece[0]].wait_recv()
            total = total + came(way, 0, piece, every)
        out[piece[1], :] = total.astype(BF16)

    for copy in started:
        copy.wait_send()


def body(nz, nx, ny, gate_q, key_k, value_v, filter_taps, skip_bias, w_out):
    channels, width = key_k.shape
    depth = w_out.shape[1]
    drows = depth // (2 * ny)
    consts = tables(nz, nx, channels // (nz * nx), width)
    vmem = lambda *shape, dtype=BF16: pltpu.VMEM(shape, dtype)
    dma = lambda *shape: pltpu.SemaphoreType.DMA(shape)
    operands = (
        gate_q, key_k, value_v, filter_taps, skip_bias.reshape(1, channels), w_out, *consts
    )
    scratch = [vmem(*a.shape, dtype=a.dtype) for a in operands]
    scratch += [
        dma(len(operands)),
        vmem(channels, width, dtype=F32),
        vmem(channels, width, dtype=F32),
        vmem(depth, channels),
        vmem(2, channels, width),
        vmem(2, channels, width),
        vmem(2, channels, width),
        vmem(2, channels, width),
        vmem(2, channels, width, dtype=F32),
        vmem(channels, width),
        vmem(channels, width),
        vmem(channels, width),
        vmem(channels, width),
        vmem(ny, drows, width),
        vmem(ny, drows, width),
        vmem(ny, drows, width, dtype=F32),
        vmem(2, 4, drows, width),
        vmem(2, 4, drows, width),
        dma(3, nz - 1), dma(3, nz - 1),
        dma(3, nx - 1), dma(3, nx - 1),
        dma(ny), dma(ny),
        dma(2, 4, ROW_PARTS), dma(2, 4, ROW_PARTS),
    ]
    return pl.pallas_call(
        functools.partial(kernel, nz, nx, ny),
        out_shape=jax.ShapeDtypeStruct((drows, width), BF16),
        in_specs=[pl.BlockSpec(memory_space=pltpu.HBM)] * len(operands),
        out_specs=pl.BlockSpec(memory_space=pltpu.VMEM),
        scratch_shapes=scratch,
        compiler_params=pltpu.CompilerParams(
            collective_id=0, has_side_effects=True, vmem_limit_bytes=40 << 20
        ),
    )(*[pltpu.with_memory_space_constraint(a, pltpu.HBM) for a in operands])


def solution(mesh):
    nz, ny = mesh.shape["ctx"] // NX, mesh.shape["tp"] // 2
    return jax.shard_map(
        functools.partial(body, nz, NX, ny),
        mesh=mesh,
        in_specs=(
            P("tp", "ctx"),
            P("tp", "ctx"),
            P("tp", "ctx"),
            P("tp", "ctx"),
            P("tp"),
            P("tp", None),
        ),
        out_specs=P("tp", "ctx"),
        check_vma=False,
    )
```
